512 devices in a mesh: lrow: 8 (over z), rcol: 16 (over x, y_lo, core), term: 4 (over y_hi).
Axes of the slice: x: 4, y: 8 (y_hi: 4, y_lo: 2; y = y_hi * 2 + y_lo), z: 8, core: 2. Of those that a mesh axis runs over, the one named last changes fastest.
Arguments:
- core_left: bfloat16 [256, 256, 128], P(None, 'rcol'), may hold values from -6 to 6
- core_right: bfloat16 [256, 256, 128], P('rcol', 'lrow'), may hold values from -0.03125 to 0.03125
- env_left: bfloat16 [20, 32, 256], P('term', 'lrow'), may hold values from -0.375 to 0.375
- env_right: bfloat16 [20, 256, 256], P('term'), may hold values from -0.375 to 0.375
- coef_left: float32 [20, 3, 128], P('term'), may hold values from -1.5 to 1.5
- coef_right: float32 [20, 3, 128], P('term'), may hold values from -1.5 to 1.5
- projected: bfloat16 [128, 32, 256, 128], P('term', 'lrow', 'rcol'), may hold values from -6 to 6
Outputs:
- residual: bfloat16 [128, 32, 256, 128], P('term', 'lrow', 'rcol')
The draws below stay inside these ranges and needn't reach their ends.
All inputs are finite; a program needn't handle non-finite values.
Results may differ from the reference program's by a relative error of at most 0.012.
Values may be sent and summed in bfloat16 or wider, within the bound.
No kernel may reach another device: no remote copies, remote signals or barrier semaphores. Data moves between devices by JAX's collectives and lax.ppermute only.
A program may use at most 64 MiB of HBM per device.

```python
import jax
import jax.numpy as jnp
from jax import lax

RANK = 256
N = 128
TERMS = 20
SLAB = 32


def block_scale(rng, dims, split, least, high):
    loudness, own = 1.0, jax.random.fold_in(rng, 6)
    for axis_at, parts in split:
        draws = jnp.exp(jax.random.uniform(jax.random.fold_in(own, axis_at), (parts,), jnp.float32, least / len(split), high / len(split)))
        loudness = loudness * jnp.repeat(draws, dims[axis_at] // parts).reshape([-1 if axis == axis_at else 1 for axis in range(len(dims))])
    return loudness


def gaussian(rng, dims, spread, bound, pieces=(), dtype=jnp.bfloat16):
    factor_of = block_scale(rng, dims, pieces, -0.22, 0.18) if pieces else 1.0
    drawn = jax.random.normal(rng, dims, jnp.float32) * spread * factor_of
    return jnp.minimum(jnp.maximum(drawn, -bound), bound).astype(dtype)


def setup_inputs(seed: int = 0) -> dict:
    keys = jax.random.split(jax.random.key(seed), 8)
    core_left = gaussian(keys[0], (RANK, RANK, N), 1.0, 6.0, ((1, 16),))
    core_right = gaussian(keys[1], (RANK, RANK, N), (8 * TERMS * RANK) ** -0.5, 0.03125, ((0, 16), (1, 8)))
    env_left = gaussian(keys[2], (TERMS, SLAB, RANK), RANK ** -0.5, 0.375, ((0, 4), (1, 8)))
    env_right = gaussian(keys[3], (TERMS, RANK, RANK), RANK ** -0.5, 0.375, ((0, 4),))
    coef_left = jnp.clip(jax.random.uniform(keys[4], (TERMS, 3, N), jnp.float32, -1.5, 1.5) * block_scale(keys[4], (TERMS, 3, N), ((0, 4),), -0.4, 0.0), -1.5, 1.5)
    coef_right = jnp.clip(jax.random.uniform(keys[5], (TERMS, 3, N), jnp.float32, -1.5, 1.5) * block_scale(keys[5], (TERMS, 3, N), ((0, 4),), -0.4, 0.0), -1.5, 1.5)
    projected = gaussian(keys[6], (N, SLAB, RANK, N), 1.0, 6.0, ((0, 4), (1, 8), (2, 16)))
    return {"core_left": core_left, "core_right": core_right, "env_left": env_left, "env_right": env_right, "coef_left": coef_left, "coef_right": coef_right, "projected": projected}


def stencil(field, coef):
    zero = jnp.zeros_like(field[..., :1])
    before = jnp.concatenate([zero, field[..., :-1]], axis=-1)
    after = jnp.concatenate([field[..., 1:], zero], axis=-1)
    return coef[0] * field + coef[1] * before + coef[2] * after


def reference(core_left, core_right, env_left, env_right, coef_left, coef_right, projected):
    left_wide = core_left.astype(jnp.float32)
    right_wide = core_right.astype(jnp.float32)

    def per_term(total, inputs):
        left_env, right_env, left_coef, right_coef = inputs
        left_field = stencil(left_wide, left_coef).astype(jnp.bfloat16)
        left_frame = jnp.einsum("pq,qrs->rps", left_env.astype(jnp.float32), left_field.astype(jnp.float32)).astype(jnp.bfloat16)
        right_field = stencil(right_wide, right_coef).astype(jnp.bfloat16)
        right_frame = jnp.einsum("bq,rqj->rbj", right_env.astype(jnp.float32), right_field.astype(jnp.float32)).astype(jnp.bfloat16)
        total = total + jnp.einsum("rai,rbj->jabi", left_frame.astype(jnp.float32), right_frame.astype(jnp.float32))
        return total, None

    start = jnp.zeros((N, SLAB, RANK, N), jnp.float32)
    total, unused = lax.scan(per_term, start, (env_left, env_right, coef_left, coef_right))
    return (projected.astype(jnp.float32) - total).astype(jnp.bfloat16)
```

```python
import jax
import jax.numpy as jnp
from jax import lax
from jax.experimental import pallas as pl
from jax.experimental.pallas import tpu as pltpu
from jax.sharding import Mesh, PartitionSpec as P

BF16, F32 = jnp.bfloat16, jnp.float32
RCOL = ("x1", "x0", "y", "core")


def spread(block, axes, count):
    return lax.all_to_all(
        jnp.broadcast_to(block[None], (count,) + block.shape), axes, 0, 0, tiled=True
    )


def frames_kernel(coef_ref, env_ref, core_ref, left_ref, out_ref, raw, frame):
    terms, points, ranks, rows = 20, 16, 128, 64
    group = 4

    def make(step, carry):
        start = pl.multiple_of(step * group * rows, group * rows)
        raw[...] = lax.dot_general(
            env_ref[pl.ds(start, group * rows), :],
            core_ref[...],
            (((1,), (1,)), ((), ())),
            preferred_element_type=F32,
        )
        for at in range(group):
            t = step * group + at
            top = at * rows
            columns = pl.ds(pl.multiple_of(t * ranks, ranks), ranks)
            for j in range(points):
                value = (
                    coef_ref[t, j] * raw[top : top + rows, (j + 1) * ranks : (j + 2) * ranks]
                    + coef_ref[t, points + j] * raw[top : top + rows, j * ranks : (j + 1) * ranks]
                    + coef_ref[t, 2 * points + j] * raw[top : top + rows, (j + 2) * ranks : (j + 3) * ranks]
                )
                frame[j * rows : (j + 1) * rows, columns] = value.astype(BF16)
        return carry

    lax.fori_loop(0, terms // group, make, 0)

    def contract(step, carry):
        start = pl.multiple_of(step * 4 * rows, 4 * rows)
        part = jnp.dot(frame[pl.ds(start, 4 * rows), :], left_ref[...], preferred_element_type=F32).astype(BF16)
        for at in range(4):
            for dest in range(4):
                for a in range(4):
                    out_ref[dest, step * 4 + at, a] = part[
                        at * rows + dest * 16 : at * rows + dest * 16 + 16, a * 128 : (a + 1) * 128
                    ]
        return carry

    lax.fori_loop(0, points // 4, contract, 0)


def frames_and_product(coef, env, core, left):
    vmem = pl.BlockSpec(memory_space=pltpu.VMEM)
    return pl.pallas_call(
        frames_kernel,
        out_shape=jax.ShapeDtypeStruct((4, 16, 4, 16, 128), BF16),
        in_specs=[pl.BlockSpec(memory_space=pltpu.SMEM), vmem, vmem, vmem],
        out_specs=vmem,
        scratch_shapes=[pltpu.VMEM((256, 18 * 128), F32), pltpu.VMEM((1024, 2560), BF16)],
        compiler_params=pltpu.CompilerParams(vmem_limit_bytes=40 << 20),
        cost_estimate=pl.CostEstimate(flops=4_200_000_000, bytes_accessed=8_000_000, transcendentals=0),
    )(coef, env, core, left)


def on_device(core_left, core_right, env_left, env_right, coef_left, coef_right, projected):
    x0, x1 = lax.axis_index("x0"), lax.axis_index("x1")
    core, term = lax.axis_index("core"), lax.axis_index("term")
    swap = [(0, 1), (1, 0)]

    points = core_right.reshape(512, 128).T
    points = jnp.pad(points, ((1, 1), (0, 0)))
    mine = lax.dynamic_slice(points, (term * 32, 0), (34, 512))
    windows = jnp.stack([mine[:18], mine[16:]]).reshape(1, 2, 72, 128)
    windows = jnp.broadcast_to(windows, (16, 2, 72, 128)).reshape(32, 72, 128)
    slices = lax.all_to_all(windows, ("lrow", "x1", "x0"), 0, 0, tiled=True)
    slices = slices.reshape(8, 4, 18, 16, 32).transpose(2, 1, 3, 0, 4).reshape(18, 64, 256)
    other = lax.ppermute(slices, "core", swap)
    second = jnp.concatenate([slices, other], axis=1).reshape(18 * 128, 256)

    small = jnp.concatenate(
        [
            env_left.astype(F32).reshape(40, 128),
            coef_left.reshape(15, 128),
            coef_right.reshape(15, 128),
            jnp.zeros((2, 128), F32),
        ]
    )
    small = spread(small, "term", 4).reshape(4, 72, 128)
    envs = small[:, :40].reshape(80, 256).astype(BF16)
    lefts = small[:, 40:55].reshape(20, 3, 1, 1, 128)
    rights = small[:, 55:70].reshape(20, 3, 128)

    raw = jnp.dot(envs, core_left.reshape(256, 2048), preferred_element_type=F32).reshape(20, 4, 16, 128)
    before = jnp.pad(raw[..., :-1], ((0, 0), (0, 0), (0, 0), (1, 0)))
    after = jnp.pad(raw[..., 1:], ((0, 0), (0, 0), (0, 0), (0, 1)))
    frame = lefts[:, 0] * raw + lefts[:, 1] * before + lefts[:, 2] * after
    frame = frame.astype(BF16).transpose(0, 2, 1, 3).reshape(20 * 16, 512)
    frame = spread(frame, ("x1", "x0"), 4)
    frame = frame.reshape(4, 20, 16, 512).transpose(1, 0, 2, 3).reshape(20, 64, 512)
    other = lax.ppermute(frame, "core", swap)
    left = jnp.concatenate([frame, other], axis=1).reshape(2560, 512)

    rows = env_right.reshape(5, 2, 4, 2, 16, 256)
    rows = lax.dynamic_slice(rows, (0, x1, 0, core, 0, 0), (5, 1, 4, 1, 16, 256)).reshape(320, 256)
    env = spread(rows, "term", 4).reshape(1280, 256)

    coef = lax.dynamic_slice(rights, (0, 0, term * 32 + x0 * 16), (20, 3, 16)).reshape(20, 48)
    part = frames_and_product(coef, env, second, left)
    part = lax.all_to_all(part, ("x0", "y"), 0, 0, tiled=True).reshape(2, 2, 16, 4, 16, 128)
    summed = (part[:, 0].astype(F32) + part[:, 1].astype(F32)).reshape(32, 4, 16, 128)
    return (projected.astype(F32) - summed).astype(BF16)


def solution(mesh):
    split = Mesh(mesh.devices.reshape(8, 2, 2, 2, 2, 4), ("lrow",) + RCOL + ("term",))
    return jax.shard_map(
        on_device,
        mesh=split,
        in_specs=(
            P(None, RCOL, None),
            P(RCOL, "lrow", None),
            P("term", "lrow", None),
            P("term", None, None),
            P("term", None, None),
            P("term", None, None),
            P("term", "lrow", RCOL, None),
        ),
        out_specs=P("term", "lrow", RCOL, None),
        check_vma=False,
    )
```

```python
import jax
import jax.numpy as jnp
from jax import lax
from jax.experimental import pallas as pl
from jax.experimental.pallas import tpu as pltpu
from jax.sharding import Mesh, PartitionSpec as P

BF16, F32 = jnp.bfloat16, jnp.float32
RCOL = ("x1", "x0", "y", "core")
VMEM = pl.BlockSpec(memory_space=pltpu.VMEM)
SMEM = pl.BlockSpec(memory_space=pltpu.SMEM)


def shifted(block, axes):
    return [lax.ppermute(block, axes, [(i, (i + shift) % 4) for i in range(4)]) for shift in range(1, 4)]


def unscramble(at, ref, core):
    lane = lax.broadcasted_iota(jnp.int32, (80, 128), 1)
    low, even = lane < 64, (lane // 32) % 2 == 0
    for x in range(4):
        for half in range(2):
            t0, t1, t2, t3 = (
                ref[((half * 4 + m) * 4 + x) * 5 : ((half * 4 + m) * 4 + x + 1) * 5].reshape(80, 128).astype(F32)
                for m in range(4)
            )
            t0, t2 = jnp.where(low, t0, pltpu.roll(t2, 64, 1)), jnp.where(low, pltpu.roll(t0, 64, 1), t2)
            t1, t3 = jnp.where(low, t1, pltpu.roll(t3, 64, 1)), jnp.where(low, pltpu.roll(t1, 64, 1), t3)
            t0, t1 = jnp.where(even, t0, pltpu.roll(t1, 32, 1)), jnp.where(even, pltpu.roll(t0, 96, 1), t1)
            t2, t3 = jnp.where(even, t2, pltpu.roll(t3, 32, 1)), jnp.where(even, pltpu.roll(t2, 96, 1), t3)
            for g, tile in enumerate((t0, t1, t2, t3)):
                tile = tile.astype(BF16)
                for jj in range(5):
                    j = jj * 4 + g
                    if j < 18:
                        top = j * 128 + at * 64 + x * 16
                        core[top : top + 16, half * 128 : half * 128 + 128] = tile[jj * 16 : jj * 16 + 16]


def main_kernel(place_ref, coef_ref, env_hbm, mine_hbm, other_hbm, l0, l1, l2, l3, m0,
                out_ref, env_ref, mine_ref, other_ref, left_ref, frame, core, raw, sem):
    points, ranks, rows, group = 16, 128, 64, 4
    own, column, term = place_ref[0] * 16, place_ref[1], place_ref[2]

    copies = [
        pltpu.make_async_copy(mine_hbm, mine_ref, sem.at[0]),
        pltpu.make_async_copy(other_hbm.at[pl.ds(0, 160)], other_ref, sem.at[1]),
    ]
    for dest in range(4):
        start = pl.multiple_of(dest * 32 + own, 16)
        copies.append(pltpu.make_async_copy(env_hbm.at[:, pl.ds(start, 16), :], env_ref.at[:, dest], sem.at[2 + dest]))
    pieces = []
    for shift, ref in enumerate((l0, l1, l2, l3)):
        top = pl.multiple_of(lax.rem(column - shift + 4, 4) * 16, 16)
        for a in range(4):
            lanes = pl.ds(a * 128, 128)
            twin = m0.at[a] if shift == 0 else other_hbm.at[pl.ds(160 + (shift - 1) * 80 + a * 20, 20)]
            at = 6 + (shift * 4 + a) * 2
            pieces.append(pltpu.make_async_copy(ref.at[a], left_ref.at[:, pl.ds(top, 16), lanes], sem.at[at]))
            pieces.append(pltpu.make_async_copy(twin, left_ref.at[:, pl.ds(top + 64, 16), lanes], sem.at[at + 1]))
    for copy in copies + pieces:
        copy.start()
    copies[0].wait()
    unscramble(0, mine_ref, core)
    copies[1].wait()
    unscramble(1, other_ref, core)
    for copy in copies[2:]:
        copy.wait()

    def make(step, carry):
        parts = []
        for at in range(group):
            t = step * group + at
            t = lax.rem(term - t // 5 + 4, 4) * 5 + lax.rem(t, 5)
            parts.append(env_ref[t].reshape(rows, 256))
        raw[...] = lax.dot_general(
            jnp.concatenate(parts, axis=0), core[...], (((1,), (1,)), ((), ())), preferred_element_type=F32
        )
        for at in range(group):
            t = step * group + at
            rows_at = slice(at * rows, (at + 1) * rows)
            columns = pl.ds(pl.multiple_of(t * ranks, ranks), ranks)
            for j in range(points):
                frame[j * rows : (j + 1) * rows, columns] = (
                    coef_ref[t, j] * raw[rows_at, (j + 1) * ranks : (j + 2) * ranks]
                    + coef_ref[t, points + j] * raw[rows_at, j * ranks : (j + 1) * ranks]
                    + coef_ref[t, 2 * points + j] * raw[rows_at, (j + 2) * ranks : (j + 3) * ranks]
                ).astype(BF16)
        return carry

    lax.fori_loop(0, 5, make, 0)
    for copy in pieces:
        copy.wait()

    def contract(step, carry):
        start = pl.multiple_of(step * 4 * rows, 4 * rows)
        part = jnp.dot(
            frame[pl.ds(start, 4 * rows), :], left_ref[...].reshape(2560, 512), preferred_element_type=F32
        ).astype(BF16)
        for at in range(4):
            for dest in range(4):
                top = at * rows + dest * 16
                for a in range(4):
                    out_ref[dest, step * 4 + at, a] = part[top : top + 16, a * 128 : (a + 1) * 128]
        return carry

    lax.fori_loop(0, points // 4, contract, 0)


def main_product(place, coef, env, mine, other, pieces):
    anywhere = pl.BlockSpec(memory_space=pl.ANY)
    return pl.pallas_call(
        main_kernel,
        out_shape=jax.ShapeDtypeStruct((4, 16, 4, 16, 128), BF16),
        in_specs=[SMEM, SMEM] + [anywhere] * 8,
        out_specs=VMEM,
        scratch_shapes=[
            pltpu.VMEM((20, 4, 16, 256), BF16),
            pltpu.VMEM((160, 16, 128), BF16),
            pltpu.VMEM((160, 16, 128), BF16),
            pltpu.VMEM((20, 128, 512), BF16),
            pltpu.VMEM((1024, 2560), BF16),
            pltpu.VMEM((18 * 128, 256), BF16),
            pltpu.VMEM((256, 18 * 128), F32),
            pltpu.SemaphoreType.DMA((38,)),
        ],
        compiler_params=pltpu.CompilerParams(vmem_limit_bytes=24 << 20),
        cost_estimate=pl.CostEstimate(flops=4_200_000_000, bytes_accessed=8_000_000, transcendentals=0),
    )(place, coef, env, mine, other, *pieces)


def on_device(core_left, core_right, env_left, env_right, coef_left, coef_right, projected):
    x0, x1 = lax.axis_index("x0"), lax.axis_index("x1")
    core, term = lax.axis_index("core"), lax.axis_index("term")
    swap = [(0, 1), (1, 0)]

    env = lax.dynamic_slice(env_right, (0, x1 * 128, 0), (5, 128, 256))
    env, core_right = lax.optimization_barrier((env, core_right))
    env = lax.all_gather(env, "term", axis=0, tiled=True)

    points = core_right.reshape(512, 128).T
    points = jnp.pad(points, ((1, 3), (0, 0)))
    mine = lax.dynamic_slice(points, (term * 32, 0), (36, 512))
    windows = jnp.stack([mine[:20], mine[16:]]).reshape(2, 5, 4, 16, 32).transpose(0, 1, 3, 2, 4)
    windows = jnp.broadcast_to(windows.reshape(1, 2, 80, 128), (16, 2, 80, 128)).reshape(32, 80, 128)
    windows, env_left = lax.optimization_barrier((windows, env_left))
    slices = lax.all_to_all(windows, ("lrow", "x1", "x0"), 0, 0, tiled=True).reshape(2560, 128)

    zero = jnp.zeros((5, 1, 128), F32)
    wide = env_left.astype(F32)
    small = jnp.concatenate([wide[..., :128], wide[..., 128:], coef_left, zero, coef_right, zero], axis=1)
    small = jnp.concatenate([small] + shifted(small, "term"))
    envs = jnp.concatenate([small[:, :4], small[:, 4:8]], axis=-1).transpose(1, 0, 2).reshape(80, 256).astype(BF16)
    lefts = small[:, 8:11].reshape(1, 20, 3, 1, 128)
    rights = small[:, 12:15]

    raw = jnp.dot(envs, core_left.reshape(256, 2048), preferred_element_type=F32).reshape(4, 20, 16, 128)
    before = jnp.pad(raw[..., :-1], ((0, 0), (0, 0), (0, 0), (1, 0)))
    after = jnp.pad(raw[..., 1:], ((0, 0), (0, 0), (0, 0), (0, 1)))
    left = lefts[:, :, 0] * raw + lefts[:, :, 1] * before + lefts[:, :, 2] * after
    left = left.astype(BF16).reshape(1280, 128)
    others = shifted(left, ("x1", "x0"))
    twin = lax.ppermute(left, "core", swap)
    slices, env, twin, *others = lax.optimization_barrier((slices, env, twin, *others))
    exchanged = lax.ppermute(jnp.concatenate([slices] + others), "core", swap)

    place = jnp.stack([core, x1 * 2 + x0, term])
    coef = lax.dynamic_slice(rights, (0, 0, term * 32 + x0 * 16), (20, 3, 16)).reshape(20, 48)
    pieces = [piece.reshape(4, 20, 16, 128) for piece in [left] + others + [twin]]
    part = main_product(
        place, coef, env, slices.reshape(160, 16, 128), exchanged.reshape(400, 16, 128), pieces
    )
    part = lax.all_to_all(part, ("x0", "y"), 0, 0, tiled=True).reshape(2, 2, 16, 4, 16, 128)
    summed = (part[:, 0].astype(F32) + part[:, 1].astype(F32)).reshape(32, 4, 16, 128)
    return (projected.astype(F32) - summed).astype(BF16)


def solution(mesh):
    split = Mesh(mesh.devices.reshape(8, 2, 2, 2, 2, 4), ("lrow",) + RCOL + ("term",))
    return jax.shard_map(
        on_device,
        mesh=split,
        in_specs=(
            P(None, RCOL, None),
            P(RCOL, "lrow", None),
            P("term", "lrow", None),
            P("term", None, None),
            P("term", None, None),
            P("term", None, None),
            P("term", "lrow", RCOL, None),
        ),
        out_specs=P("term", "lrow", RCOL, None),
        check_vma=False,
    )
```

```python
import jax
import jax.numpy as jnp
from jax import lax
from jax.experimental import pallas as pl
from jax.experimental.pallas import tpu as pltpu
from jax.sharding import Mesh, PartitionSpec as P

BF16, F32 = jnp.bfloat16, jnp.float32
RCOL = ("x1", "x0", "y", "core")
VMEM = pl.BlockSpec(memory_space=pltpu.VMEM)
SMEM = pl.BlockSpec(memory_space=pltpu.SMEM)


def shifted(block, axes):
    return [lax.ppermute(block, axes, [(i, (i + shift) % 4) for i in range(4)]) for shift in range(1, 4)]


def unscramble(at, ref, core):
    lane = lax.broadcasted_iota(jnp.int32, (80, 128), 1)
    low, even = lane < 64, (lane // 32) % 2 == 0
    for x in range(4):
        for half in range(2):
            t0, t1, t2, t3 = (
                ref[((half * 4 + m) * 4 + x) * 5 : ((half * 4 + m) * 4 + x + 1) * 5].reshape(80, 128).astype(F32)
                for m in range(4)
            )
            t0, t2 = jnp.where(low, t0, pltpu.roll(t2, 64, 1)), jnp.where(low, pltpu.roll(t0, 64, 1), t2)
            t1, t3 = jnp.where(low, t1, pltpu.roll(t3, 64, 1)), jnp.where(low, pltpu.roll(t1, 64, 1), t3)
            t0, t1 = jnp.where(even, t0, pltpu.roll(t1, 32, 1)), jnp.where(even, pltpu.roll(t0, 96, 1), t1)
            t2, t3 = jnp.where(even, t2, pltpu.roll(t3, 32, 1)), jnp.where(even, pltpu.roll(t2, 96, 1), t3)
            for g, tile in enumerate((t0, t1, t2, t3)):
                tile = tile.astype(BF16)
                for jj in range(5):
                    j = jj * 4 + g
                    if j < 18:
                        top = j * 128 + at * 64 + x * 16
                        core[top : top + 16, half * 128 : half * 128 + 128] = tile[jj * 16 : jj * 16 + 16]


def frames_kernel(
    coef_ref, shared_hbm, mine_hbm, other_hbm, frame_hbm, token_ref, frame, env_ref, mine_ref, other_ref, core, raw, sem
):
    points, ranks, rows, group = 16, 128, 64, 4
    copies = [
        pltpu.make_async_copy(mine_hbm, mine_ref, sem.at[0]),
        pltpu.make_async_copy(other_hbm, other_ref, sem.at[1]),
    ]
    for t in range(4):
        for half in range(2):
            copies.append(
                pltpu.make_async_copy(
                    shared_hbm.at[t, pl.ds(half * 320, 320)],
                    env_ref.at[pl.ds(t * 320, 320), pl.ds(half * 128, 128)],
                    sem.at[2 + t * 2 + half],
                )
            )
    for copy in copies:
        copy.start()
    copies[0].wait()
    unscramble(0, mine_ref, core)
    copies[1].wait()
    unscramble(1, other_ref, core)
    for copy in copies[2:]:
        copy.wait()

    def make(step, carry):
        start = pl.multiple_of(step * group * rows, group * rows)
        env = env_ref[pl.ds(start, group * rows), :]
        raw[...] = lax.dot_general(env, core[...], (((1,), (1,)), ((), ())), preferred_element_type=F32)
        for at in range(group):
            t = step * group + at
            rows_at = slice(at * rows, (at + 1) * rows)
            columns = pl.ds(pl.multiple_of(t * ranks, ranks), ranks)
            for j in range(points):
                frame[j * rows : (j + 1) * rows, columns] = (
                    coef_ref[t, j] * raw[rows_at, (j + 1) * ranks : (j + 2) * ranks]
                    + coef_ref[t, points + j] * raw[rows_at, j * ranks : (j + 1) * ranks]
                    + coef_ref[t, 2 * points + j] * raw[rows_at, (j + 2) * ranks : (j + 3) * ranks]
                ).astype(BF16)
        out(step).start()
        return carry

    def out(step):
        columns = pl.ds(pl.multiple_of(step * group * ranks, group * ranks), group * ranks)
        return pltpu.make_async_copy(frame.at[:, columns], frame_hbm.at[:, columns], sem.at[10 + step])

    lax.fori_loop(0, 5, make, 0)
    token_ref[...] = raw[:8, :128]
    for step in range(5):
        out(step).wait()


def product_kernel(place_ref, frame_hbm, l0, l1, l2, l3, far_hbm, token, out_ref, left_ref, frame, sem):
    column = place_ref[0]
    pieces = []
    for shift, ref in enumerate((l0, l1, l2, l3)):
        top = pl.multiple_of(lax.rem(column - shift + 4, 4) * 16, 16)
        for a in range(4):
            lanes = pl.ds(a * 128, 128)
            for move, source in enumerate((ref, far_hbm.at[shift])):
                target = left_ref.at[:, pl.ds(top + move * 64, 16), lanes]
                pieces.append(pltpu.make_async_copy(source.at[a], target, sem.at[(shift * 4 + a) * 2 + move]))
    chunks = [
        pltpu.make_async_copy(frame_hbm.at[pl.ds(at * 256, 256)], frame.at[pl.ds(at * 256, 256)], sem.at[32 + at])
        for at in range(4)
    ]
    for copy in pieces + chunks:
        copy.start()
    for copy in pieces:
        copy.wait()

    def contract(step, carry):
        start = pl.multiple_of(step * 256, 256)
        pltpu.make_async_copy(frame_hbm.at[pl.ds(start, 256)], frame.at[pl.ds(start, 256)], sem.at[32 + step]).wait()
        part = jnp.dot(
            frame[pl.ds(start, 256), :], left_ref[...].reshape(2560, 512), preferred_element_type=F32
        ).astype(BF16)
        for at in range(4):
            for dest in range(4):
                top = at * 64 + dest * 16
                for a in range(4):
                    out_ref[dest, step * 4 + at, a] = part[top : top + 16, a * 128 : (a + 1) * 128]
        return carry

    lax.fori_loop(0, 4, contract, 0)


def left_kernel(shared_ref, core_ref, out_ref, coef_ref, tall):
    cores = jnp.swapaxes(core_ref[...].astype(F32), 0, 1).astype(BF16)
    lane = lax.broadcasted_iota(jnp.int32, (80, 128), 1)
    totals = []
    for t in range(4):
        total = (
            shared_ref[t, 680:710].astype(F32) + shared_ref[t, 710:740].astype(F32) + shared_ref[t, 740:770].astype(F32)
        )
        coef_ref[t] = total[15:]
        totals.append(total)
    envs = []
    for a in range(4):
        for t in range(4):
            rows = shared_ref[t, 640:680].astype(F32)
            envs.append(jnp.concatenate([rows[a * 5 : a * 5 + 5], rows[20 + a * 5 : 25 + a * 5]], axis=1))
    envs = jnp.concatenate(envs, axis=0).astype(BF16)
    scales = [[total[k * 5 : k * 5 + 5] for total in totals] * 4 for k in range(3)]
    centre, lower, upper = (jnp.concatenate(part, axis=0) for part in scales)
    lower = jnp.where(lane == 0, 0.0, lower)
    upper = jnp.where(lane == 127, 0.0, upper)
    for r in range(16):
        raw = jnp.dot(envs, cores[r], preferred_element_type=F32)
        tall[pl.ds(r, 80, stride=16), :] = (
            centre * raw + lower * pltpu.roll(raw, 1, 1) + upper * pltpu.roll(raw, 127, 1)
        )
    out_ref[...] = tall[...].astype(BF16)


def left_frames(shared, core):
    return pl.pallas_call(
        left_kernel,
        out_shape=(jax.ShapeDtypeStruct((1280, 128), BF16), jax.ShapeDtypeStruct((4, 15, 128), F32)),
        in_specs=[VMEM, VMEM],
        out_specs=(VMEM, VMEM),
        scratch_shapes=[pltpu.VMEM((1280, 128), F32)],
        compiler_params=pltpu.CompilerParams(vmem_limit_bytes=8 << 20),
        cost_estimate=pl.CostEstimate(flops=84_000_000, bytes_accessed=2_000_000, transcendentals=0),
    )(shared, core)


ANYWHERE = pl.BlockSpec(memory_space=pl.ANY)
HBM = pl.BlockSpec(memory_space=pltpu.HBM)


def right_frames(coef, shared, mine, other):
    return pl.pallas_call(
        frames_kernel,
        out_shape=(jax.ShapeDtypeStruct((1024, 2560), BF16), jax.ShapeDtypeStruct((8, 128), F32)),
        in_specs=[SMEM] + [ANYWHERE] * 3,
        out_specs=(HBM, VMEM),
        scratch_shapes=[
            pltpu.VMEM((1024, 2560), BF16),
            pltpu.VMEM((1280, 256), BF16),
            pltpu.VMEM((160, 16, 128), BF16),
            pltpu.VMEM((160, 16, 128), BF16),
            pltpu.VMEM((18 * 128, 256), BF16),
            pltpu.VMEM((256, 18 * 128), F32),
            pltpu.SemaphoreType.DMA((15,)),
        ],
        compiler_params=pltpu.CompilerParams(vmem_limit_bytes=52 << 20),
        cost_estimate=pl.CostEstimate(flops=1_500_000_000, bytes_accessed=8_000_000, transcendentals=0),
    )(coef, shared, mine, other)


def product(place, frame, pieces):
    return pl.pallas_call(
        product_kernel,
        out_shape=jax.ShapeDtypeStruct((4, 16, 4, 16, 128), BF16),
        in_specs=[SMEM, HBM] + [ANYWHERE] * 6,
        out_specs=VMEM,
        scratch_shapes=[
            pltpu.VMEM((20, 128, 512), BF16),
            pltpu.VMEM((1024, 2560), BF16),
            pltpu.SemaphoreType.DMA((36,)),
        ],
        compiler_params=pltpu.CompilerParams(vmem_limit_bytes=52 << 20),
        cost_estimate=pl.CostEstimate(flops=2_700_000_000, bytes_accessed=8_000_000, transcendentals=0),
    )(place, frame, *pieces)


def on_device(core_left, core_right, env_left, env_right, coef_left, coef_right, projected):
    x0, x1 = lax.axis_index("x0"), lax.axis_index("x1")
    core, term = lax.axis_index("core"), lax.axis_index("term")
    swap = [(0, 1), (1, 0)]

    env = env_right.reshape(5, 2, 4, 2, 16, 256)
    env = lax.dynamic_slice(env, (0, x1, 0, core, 0, 0), (5, 1, 4, 1, 16, 256)).reshape(320, 256)
    coefs = jnp.concatenate([coef_left.transpose(1, 0, 2).reshape(15, 128), coef_right.reshape(15, 128)])
    high = lax.reduce_precision(coefs, 8, 7)
    middle = lax.reduce_precision(coefs - high, 8, 7)
    low = coefs - high - middle
    envs = env_left.transpose(1, 0, 2).reshape(20, 256)
    shared = jnp.concatenate(
        [env[:, :128], env[:, 128:], envs[:, :128], envs[:, 128:]]
        + [part.astype(BF16) for part in (high, middle, low)]
        + [jnp.zeros((14, 128), BF16)]
    )
    shared = lax.all_gather(shared, "term")

    points = core_right.reshape(512, 128).T
    points = jnp.pad(points, ((1, 3), (0, 0)))
    mine = lax.dynamic_slice(points, (term * 32, 0), (36, 512))
    windows = jnp.stack([mine[:20], mine[16:]]).reshape(2, 5, 4, 16, 32).transpose(0, 1, 3, 2, 4)
    windows = jnp.broadcast_to(windows.reshape(1, 2, 80, 128), (16, 2, 80, 128)).reshape(32, 80, 128)
    slices = lax.all_to_all(windows, ("lrow", "x1", "x0"), 0, 0, tiled=True).reshape(2560, 128)

    left, rights = left_frames(shared, core_left)
    others = shifted(left, ("x1", "x0"))
    slices, left = lax.optimization_barrier((slices, left))
    other = lax.ppermute(slices, "core", swap)
    coef = lax.dynamic_slice(rights.reshape(20, 3, 128), (0, 0, term * 32 + x0 * 16), (20, 3, 16)).reshape(20, 48)
    frame, token = right_frames(coef, shared, slices.reshape(160, 16, 128), other.reshape(160, 16, 128))
    token, others = lax.optimization_barrier((token, others))
    twins = lax.ppermute(jnp.concatenate([left] + others), "core", swap).reshape(4, 4, 20, 16, 128)
    pieces = [piece.reshape(4, 20, 16, 128) for piece in [left] + others]
    part = product((x1 * 2 + x0).reshape(1), frame, pieces + [twins, token])
    part = lax.all_to_all(part, ("x0", "y"), 0, 0, tiled=True).reshape(2, 2, 16, 4, 16, 128)
    summed = (part[:, 0].astype(F32) + part[:, 1].astype(F32)).reshape(32, 4, 16, 128)
    return (projected.astype(F32) - summed).astype(BF16)


def solution(mesh):
    split = Mesh(mesh.devices.reshape(8, 2, 2, 2, 2, 4), ("lrow",) + RCOL + ("term",))
    return jax.shard_map(
        on_device,
        mesh=split,
        in_specs=(
            P(None, RCOL, None),
            P(RCOL, "lrow", None),
            P("term", "lrow", None),
            P("term", None, None),
            P("term", None, None),
            P("term", None, None),
            P("term", "lrow", RCOL, None),
        ),
        out_specs=P("term", "lrow", RCOL, None),
        check_vma=False,
    )
```

```python
import jax
import jax.numpy as jnp
from jax import lax
from jax.experimental import pallas as pl
from jax.experimental.pallas import tpu as pltpu
from jax.sharding import Mesh, PartitionSpec as P

BF16, F32 = jnp.bfloat16, jnp.float32
RCOL = ("x1", "x0", "y", "core")
VMEM = pl.BlockSpec(memory_space=pltpu.VMEM)
SMEM = pl.BlockSpec(memory_space=pltpu.SMEM)


def unscramble(at, ref, core):
    lane = lax.broadcasted_iota(jnp.int32, (80, 128), 1)
    low, even = lane < 64, (lane // 32) % 2 == 0
    for x in range(4):
        for half in range(2):
            t0, t1, t2, t3 = (
                ref[((half * 4 + m) * 4 + x) * 5 : ((half * 4 + m) * 4 + x + 1) * 5].reshape(80, 128).astype(F32)
                for m in range(4)
            )
            t0, t2 = jnp.where(low, t0, pltpu.roll(t2, 64, 1)), jnp.where(low, pltpu.roll(t0, 64, 1), t2)
            t1, t3 = jnp.where(low, t1, pltpu.roll(t3, 64, 1)), jnp.where(low, pltpu.roll(t1, 64, 1), t3)
            t0, t1 = jnp.where(even, t0, pltpu.roll(t1, 32, 1)), jnp.where(even, pltpu.roll(t0, 96, 1), t1)
            t2, t3 = jnp.where(even, t2, pltpu.roll(t3, 32, 1)), jnp.where(even, pltpu.roll(t2, 96, 1), t3)
            for g, tile in enumerate((t0, t1, t2, t3)):
                tile = tile.astype(BF16)
                for jj in range(5):
                    j = jj * 4 + g
                    if j < 18:
                        top = j * 128 + at * 64 + x * 16
                        core[top : top + 16, half * 128 : half * 128 + 128] = tile[jj * 16 : jj * 16 + 16]


def frames_kernel(
    coef_ref, shared_hbm, mine_hbm, other_hbm, frame_hbm, token_ref, frame, env_ref, mine_ref, other_ref, core, raw, sem
):
    points, ranks, rows, group = 16, 128, 64, 4
    copies = [
        pltpu.make_async_copy(mine_hbm, mine_ref, sem.at[0]),
        pltpu.make_async_copy(other_hbm, other_ref, sem.at[1]),
    ]
    for t in range(4):
        for half in range(2):
            copies.append(
                pltpu.make_async_copy(
                    shared_hbm.at[t, pl.ds(half * 320, 320)],
                    env_ref.at[pl.ds(t * 320, 320), pl.ds(half * 128, 128)],
                    sem.at[2 + t * 2 + half],
                )
            )
    for copy in copies:
        copy.start()
    copies[0].wait()
    unscramble(0, mine_ref, core)
    copies[1].wait()
    unscramble(1, other_ref, core)
    for copy in copies[2:]:
        copy.wait()

    def make(step, carry):
        start = pl.multiple_of(step * group * rows, group * rows)
        env = env_ref[pl.ds(start, group * rows), :]
        raw[...] = lax.dot_general(env, core[...], (((1,), (1,)), ((), ())), preferred_element_type=F32)
        for at in range(group):
            t = step * group + at
            rows_at = slice(at * rows, (at + 1) * rows)
            columns = pl.ds(pl.multiple_of(t * ranks, ranks), ranks)
            for j in range(points):
                frame[j * rows : (j + 1) * rows, columns] = (
                    coef_ref[t, j] * raw[rows_at, (j + 1) * ranks : (j + 2) * ranks]
                    + coef_ref[t, points + j] * raw[rows_at, j * ranks : (j + 1) * ranks]
                    + coef_ref[t, 2 * points + j] * raw[rows_at, (j + 2) * ranks : (j + 3) * ranks]
                ).astype(BF16)
        out(step).start()
        return carry

    def out(step):
        columns = pl.ds(pl.multiple_of(step * group * ranks, group * ranks), group * ranks)
        return pltpu.make_async_copy(frame.at[:, columns], frame_hbm.at[:, columns], sem.at[10 + step])

    lax.fori_loop(0, 5, make, 0)
    token_ref[...] = raw[:8, :128]
    for step in range(5):
        out(step).wait()


def product_kernel(frame_hbm, mine_hbm, twin_hbm, token, out_ref, left_ref, frame, sem):
    pieces = []
    for x in range(4):
        for a in range(4):
            for move, source in enumerate((mine_hbm, twin_hbm)):
                target = left_ref.at[:, pl.ds(move * 64 + x * 16, 16), pl.ds(a * 128, 128)]
                pieces.append(pltpu.make_async_copy(source.at[x, a], target, sem.at[(x * 4 + a) * 2 + move]))
    chunks = [
        pltpu.make_async_copy(frame_hbm.at[pl.ds(at * 256, 256)], frame.at[pl.ds(at * 256, 256)], sem.at[32 + at])
        for at in range(4)
    ]
    for copy in pieces + chunks:
        copy.start()
    for copy in pieces:
        copy.wait()

    def contract(step, carry):
        start = pl.multiple_of(step * 256, 256)
        pltpu.make_async_copy(frame_hbm.at[pl.ds(start, 256)], frame.at[pl.ds(start, 256)], sem.at[32 + step]).wait()
        part = jnp.dot(
            frame[pl.ds(start, 256), :], left_ref[...].reshape(2560, 512), preferred_element_type=F32
        ).astype(BF16)
        for at in range(4):
            for dest in range(4):
                top = at * 64 + dest * 16
                for a in range(4):
                    out_ref[dest, step * 4 + at, a] = part[top : top + 16, a * 128 : (a + 1) * 128]
        return carry

    lax.fori_loop(0, 4, contract, 0)


def left_kernel(shared_ref, core_ref, out_ref, coef_ref, tall):
    cores = jnp.swapaxes(core_ref[...].astype(F32), 0, 1).astype(BF16)
    lane = lax.broadcasted_iota(jnp.int32, (80, 128), 1)
    totals = []
    for t in range(4):
        total = (
            shared_ref[t, 680:710].astype(F32) + shared_ref[t, 710:740].astype(F32) + shared_ref[t, 740:770].astype(F32)
        )
        coef_ref[t] = total[15:]
        totals.append(total)
    envs = []
    for a in range(4):
        for t in range(4):
            rows = shared_ref[t, 640:680].astype(F32)
            envs.append(jnp.concatenate([rows[a * 5 : a * 5 + 5], rows[20 + a * 5 : 25 + a * 5]], axis=1))
    envs = jnp.concatenate(envs, axis=0).astype(BF16)
    scales = [[total[k * 5 : k * 5 + 5] for total in totals] * 4 for k in range(3)]
    centre, lower, upper = (jnp.concatenate(part, axis=0) for part in scales)
    lower = jnp.where(lane == 0, 0.0, lower)
    upper = jnp.where(lane == 127, 0.0, upper)
    for r in range(16):
        raw = jnp.dot(envs, cores[r], preferred_element_type=F32)
        tall[pl.ds(r, 80, stride=16), :] = (
            centre * raw + lower * pltpu.roll(raw, 1, 1) + upper * pltpu.roll(raw, 127, 1)
        )
    out_ref[...] = tall[...].astype(BF16)


def left_frames(shared, core):
    return pl.pallas_call(
        left_kernel,
        out_shape=(jax.ShapeDtypeStruct((1280, 128), BF16), jax.ShapeDtypeStruct((4, 15, 128), F32)),
        in_specs=[VMEM, VMEM],
        out_specs=(VMEM, VMEM),
        scratch_shapes=[pltpu.VMEM((1280, 128), F32)],
        compiler_params=pltpu.CompilerParams(vmem_limit_bytes=8 << 20),
        cost_estimate=pl.CostEstimate(flops=84_000_000, bytes_accessed=2_000_000, transcendentals=0),
    )(shared, core)


ANYWHERE = pl.BlockSpec(memory_space=pl.ANY)
HBM = pl.BlockSpec(memory_space=pltpu.HBM)


def right_frames(coef, shared, mine, other):
    return pl.pallas_call(
        frames_kernel,
        out_shape=(jax.ShapeDtypeStruct((1024, 2560), BF16), jax.ShapeDtypeStruct((8, 128), F32)),
        in_specs=[SMEM] + [ANYWHERE] * 3,
        out_specs=(HBM, VMEM),
        scratch_shapes=[
            pltpu.VMEM((1024, 2560), BF16),
            pltpu.VMEM((1280, 256), BF16),
            pltpu.VMEM((160, 16, 128), BF16),
            pltpu.VMEM((160, 16, 128), BF16),
            pltpu.VMEM((18 * 128, 256), BF16),
            pltpu.VMEM((256, 18 * 128), F32),
            pltpu.SemaphoreType.DMA((15,)),
        ],
        compiler_params=pltpu.CompilerParams(vmem_limit_bytes=52 << 20),
        cost_estimate=pl.CostEstimate(flops=1_500_000_000, bytes_accessed=8_000_000, transcendentals=0),
    )(coef, shared, mine, other)


def product(frame, mine, twin, token):
    return pl.pallas_call(
        product_kernel,
        out_shape=jax.ShapeDtypeStruct((4, 16, 4, 16, 128), BF16),
        in_specs=[HBM] + [ANYWHERE] * 3,
        out_specs=VMEM,
        scratch_shapes=[
            pltpu.VMEM((20, 128, 512), BF16),
            pltpu.VMEM((1024, 2560), BF16),
            pltpu.SemaphoreType.DMA((36,)),
        ],
        compiler_params=pltpu.CompilerParams(vmem_limit_bytes=52 << 20),
        cost_estimate=pl.CostEstimate(flops=2_700_000_000, bytes_accessed=8_000_000, transcendentals=0),
    )(frame, mine, twin, token)


def on_device(core_left, core_right, env_left, env_right, coef_left, coef_right, projected):
    x0, x1 = lax.axis_index("x0"), lax.axis_index("x1")
    core, term = lax.axis_index("core"), lax.axis_index("term")
    swap = [(0, 1), (1, 0)]

    env = env_right.reshape(5, 2, 4, 2, 16, 256)
    env = lax.dynamic_slice(env, (0, x1, 0, core, 0, 0), (5, 1, 4, 1, 16, 256)).reshape(320, 256)
    coefs = jnp.concatenate([coef_left.transpose(1, 0, 2).reshape(15, 128), coef_right.reshape(15, 128)])
    high = lax.reduce_precision(coefs, 8, 7)
    middle = lax.reduce_precision(coefs - high, 8, 7)
    low = coefs - high - middle
    envs = env_left.transpose(1, 0, 2).reshape(20, 256)
    shared = jnp.concatenate(
        [env[:, :128], env[:, 128:], envs[:, :128], envs[:, 128:]]
        + [part.astype(BF16) for part in (high, middle, low)]
        + [jnp.zeros((14, 128), BF16)]
    )
    shared = lax.all_gather(shared, "term")

    points = core_right.reshape(512, 128).T
    points = jnp.pad(points, ((1, 3), (0, 0)))
    mine = lax.dynamic_slice(points, (term * 32, 0), (36, 512))
    windows = jnp.stack([mine[:20], mine[16:]]).reshape(2, 5, 4, 16, 32).transpose(0, 1, 3, 2, 4)
    windows = jnp.broadcast_to(windows.reshape(1, 2, 80, 128), (16, 2, 80, 128)).reshape(32, 80, 128)
    slices = lax.all_to_all(windows, ("lrow", "x1", "x0"), 0, 0, tiled=True).reshape(2560, 128)

    left, rights = left_frames(shared, core_left)
    lefts = lax.all_to_all(jnp.broadcast_to(left[None], (4, 1280, 128)), ("x1", "x0"), 0, 0, tiled=True)
    slices, left = lax.optimization_barrier((slices, left))
    other = lax.ppermute(slices, "core", swap)
    coef = lax.dynamic_slice(rights.reshape(20, 3, 128), (0, 0, term * 32 + x0 * 16), (20, 3, 16)).reshape(20, 48)
    frame, token = right_frames(coef, shared, slices.reshape(160, 16, 128), other.reshape(160, 16, 128))
    token, lefts = lax.optimization_barrier((token, lefts))
    twins = lax.ppermute(lefts, "core", swap)
    part = product(frame, lefts.reshape(4, 4, 20, 16, 128), twins.reshape(4, 4, 20, 16, 128), token)
    part = lax.all_to_all(part, ("x0", "y"), 0, 0, tiled=True).reshape(2, 2, 16, 4, 16, 128)
    summed = (part[:, 0].astype(F32) + part[:, 1].astype(F32)).reshape(32, 4, 16, 128)
    return (projected.astype(F32) - summed).astype(BF16)


def solution(mesh):
    split = Mesh(mesh.devices.reshape(8, 2, 2, 2, 2, 4), ("lrow",) + RCOL + ("term",))
    return jax.shard_map(
        on_device,
        mesh=split,
        in_specs=(
            P(None, RCOL, None),
            P(RCOL, "lrow", None),
            P("term", "lrow", None),
            P("term", None, None),
            P("term", None, None),
            P("term", None, None),
            P("term", "lrow", RCOL, None),
        ),
        out_specs=P("term", "lrow", RCOL, None),
        check_vma=False,
    )
```

```python
import jax
import jax.numpy as jnp
from jax import lax
from jax.experimental import pallas as pl
from jax.experimental.pallas import tpu as pltpu
from jax.sharding import Mesh, PartitionSpec as P

BF16, F32 = jnp.bfloat16, jnp.float32
RCOL = ("x1", "x0", "y", "core")
VMEM = pl.BlockSpec(memory_space=pltpu.VMEM)
SMEM = pl.BlockSpec(memory_space=pltpu.SMEM)


def unscramble(at, ref, core):
    lane = lax.broadcasted_iota(jnp.int32, (80, 128), 1)
    low, even = lane < 64, (lane // 32) % 2 == 0
    for x in range(4):
        for half in range(2):
            t0, t1, t2, t3 = (
                ref[((half * 4 + m) * 4 + x) * 5 : ((half * 4 + m) * 4 + x + 1) * 5].reshape(80, 128).astype(F32)
                for m in range(4)
            )
            t0, t2 = jnp.where(low, t0, pltpu.roll(t2, 64, 1)), jnp.where(low, pltpu.roll(t0, 64, 1), t2)
            t1, t3 = jnp.where(low, t1, pltpu.roll(t3, 64, 1)), jnp.where(low, pltpu.roll(t1, 64, 1), t3)
            t0, t1 = jnp.where(even, t0, pltpu.roll(t1, 32, 1)), jnp.where(even, pltpu.roll(t0, 96, 1), t1)
            t2, t3 = jnp.where(even, t2, pltpu.roll(t3, 32, 1)), jnp.where(even, pltpu.roll(t2, 96, 1), t3)
            for g, tile in enumerate((t0, t1, t2, t3)):
                tile = tile.astype(BF16)
                for jj in range(5):
                    j = jj * 4 + g
                    if j < 18:
                        top = j * 128 + at * 64 + x * 16
                        core[top : top + 16, half * 128 : half * 128 + 128] = tile[jj * 16 : jj * 16 + 16]


def frames_kernel(
    coef_ref, shared_hbm, mine_hbm, other_hbm, frame_hbm, token_ref, frame, env_ref, mine_ref, other_ref, core, raw, sem
):
    points, ranks, rows, group = 16, 128, 64, 4
    copies = [
        pltpu.make_async_copy(mine_hbm, mine_ref, sem.at[0]),
        pltpu.make_async_copy(other_hbm, other_ref, sem.at[1]),
    ]
    for t in range(4):
        for half in range(2):
            copies.append(
                pltpu.make_async_copy(
                    shared_hbm.at[t, pl.ds(half * 320, 320)],
                    env_ref.at[pl.ds(t * 320, 320), pl.ds(half * 128, 128)],
                    sem.at[2 + t * 2 + half],
                )
            )
    for copy in copies:
        copy.start()
    copies[0].wait()
    unscramble(0, mine_ref, core)
    copies[1].wait()
    unscramble(1, other_ref, core)
    for copy in copies[2:]:
        copy.wait()

    def make(step, carry):
        start = pl.multiple_of(step * group * rows, group * rows)
        env = env_ref[pl.ds(start, group * rows), :]
        raw[...] = lax.dot_general(env, core[...], (((1,), (1,)), ((), ())), preferred_element_type=F32)
        for at in range(group):
            t = step * group + at
            rows_at = slice(at * rows, (at + 1) * rows)
            columns = pl.ds(pl.multiple_of(t * ranks, ranks), ranks)
            for j in range(points):
                frame[j * rows : (j + 1) * rows, columns] = (
                    coef_ref[t, j] * raw[rows_at, (j + 1) * ranks : (j + 2) * ranks]
                    + coef_ref[t, points + j] * raw[rows_at, j * ranks : (j + 1) * ranks]
                    + coef_ref[t, 2 * points + j] * raw[rows_at, (j + 2) * ranks : (j + 3) * ranks]
                ).astype(BF16)
        out(step).start()
        return carry

    def out(step):
        columns = pl.ds(pl.multiple_of(step * group * ranks, group * ranks), group * ranks)
        return pltpu.make_async_copy(frame.at[:, columns], frame_hbm.at[:, columns], sem.at[10 + step])

    lax.fori_loop(0, 5, make, 0)
    token_ref[...] = raw[:8, :128]
    for step in range(5):
        out(step).wait()


def product_kernel(frame_hbm, mine_ref, twin_ref, projected_hbm, token, out_ref, kept_ref, left_ref, frame, sem):
    keep = pltpu.make_async_copy(projected_hbm, kept_ref, sem.at[36])
    pieces = []
    for x in range(4):
        for a in range(4):
            for move, source in enumerate((mine_ref, twin_ref)):
                target = left_ref.at[:, pl.ds(move * 64 + x * 16, 16), pl.ds(a * 128, 128)]
                pieces.append(pltpu.make_async_copy(source.at[x, a], target, sem.at[(x * 4 + a) * 2 + move]))
    chunks = [
        pltpu.make_async_copy(frame_hbm.at[pl.ds(at * 256, 256)], frame.at[pl.ds(at * 256, 256)], sem.at[32 + at])
        for at in range(4)
    ]
    for copy in pieces + chunks + [keep]:
        copy.start()
    for copy in pieces:
        copy.wait()

    def contract(step, carry):
        start = pl.multiple_of(step * 256, 256)
        pltpu.make_async_copy(frame_hbm.at[pl.ds(start, 256)], frame.at[pl.ds(start, 256)], sem.at[32 + step]).wait()
        part = jnp.dot(
            frame[pl.ds(start, 256), :], left_ref[...].reshape(2560, 512), preferred_element_type=F32
        ).astype(BF16)
        for at in range(4):
            for dest in range(4):
                top = at * 64 + dest * 16
                for a in range(4):
                    out_ref[dest, step * 4 + at, a] = part[top : top + 16, a * 128 : (a + 1) * 128]
        return carry

    lax.fori_loop(0, 4, contract, 0)
    keep.wait()


def left_kernel(shared_ref, core_ref, out_ref, coef_ref, tall):
    cores = jnp.swapaxes(core_ref[...].astype(F32), 0, 1).astype(BF16)
    lane = lax.broadcasted_iota(jnp.int32, (80, 128), 1)
    totals = []
    for t in range(4):
        total = (
            shared_ref[t, 680:710].astype(F32) + shared_ref[t, 710:740].astype(F32) + shared_ref[t, 740:770].astype(F32)
        )
        coef_ref[t] = total[15:]
        totals.append(total)
    envs = []
    for a in range(4):
        for t in range(4):
            rows = shared_ref[t, 640:680].astype(F32)
            envs.append(jnp.concatenate([rows[a * 5 : a * 5 + 5], rows[20 + a * 5 : 25 + a * 5]], axis=1))
    envs = jnp.concatenate(envs, axis=0).astype(BF16)
    scales = [[total[k * 5 : k * 5 + 5] for total in totals] * 4 for k in range(3)]
    centre, lower, upper = (jnp.concatenate(part, axis=0) for part in scales)
    lower = jnp.where(lane == 0, 0.0, lower)
    upper = jnp.where(lane == 127, 0.0, upper)
    for r in range(16):
        raw = jnp.dot(envs, cores[r], preferred_element_type=F32)
        tall[pl.ds(r, 80, stride=16), :] = (
            centre * raw + lower * pltpu.roll(raw, 1, 1) + upper * pltpu.roll(raw, 127, 1)
        )
    out_ref[...] = tall[...].astype(BF16)


def left_frames(shared, core):
    return pl.pallas_call(
        left_kernel,
        out_shape=(jax.ShapeDtypeStruct((1280, 128), BF16), jax.ShapeDtypeStruct((4, 15, 128), F32)),
        in_specs=[VMEM, VMEM],
        out_specs=(VMEM, VMEM),
        scratch_shapes=[pltpu.VMEM((1280, 128), F32)],
        compiler_params=pltpu.CompilerParams(vmem_limit_bytes=8 << 20),
        cost_estimate=pl.CostEstimate(flops=84_000_000, bytes_accessed=2_000_000, transcendentals=0),
    )(shared, core)


ANYWHERE = pl.BlockSpec(memory_space=pl.ANY)
HBM = pl.BlockSpec(memory_space=pltpu.HBM)


def right_frames(coef, shared, mine, other):
    return pl.pallas_call(
        frames_kernel,
        out_shape=(jax.ShapeDtypeStruct((1024, 2560), BF16), jax.ShapeDtypeStruct((8, 128), F32)),
        in_specs=[SMEM] + [ANYWHERE] * 3,
        out_specs=(HBM, VMEM),
        scratch_shapes=[
            pltpu.VMEM((1024, 2560), BF16),
            pltpu.VMEM((1280, 256), BF16),
            pltpu.VMEM((160, 16, 128), BF16),
            pltpu.VMEM((160, 16, 128), BF16),
            pltpu.VMEM((18 * 128, 256), BF16),
            pltpu.VMEM((256, 18 * 128), F32),
            pltpu.SemaphoreType.DMA((15,)),
        ],
        compiler_params=pltpu.CompilerParams(vmem_limit_bytes=52 << 20),
        cost_estimate=pl.CostEstimate(flops=1_500_000_000, bytes_accessed=8_000_000, transcendentals=0),
    )(coef, shared, mine, other)


def product(frame, mine, twin, projected, token):
    return pl.pallas_call(
        product_kernel,
        out_shape=(
            jax.ShapeDtypeStruct((4, 16, 4, 16, 128), BF16),
            jax.ShapeDtypeStruct((32, 4, 16, 128), BF16),
        ),
        in_specs=[HBM, ANYWHERE, ANYWHERE, HBM, ANYWHERE],
        out_specs=(VMEM, VMEM),
        scratch_shapes=[
            pltpu.VMEM((20, 128, 512), BF16),
            pltpu.VMEM((1024, 2560), BF16),
            pltpu.SemaphoreType.DMA((37,)),
        ],
        compiler_params=pltpu.CompilerParams(vmem_limit_bytes=46 << 20),
        cost_estimate=pl.CostEstimate(flops=2_700_000_000, bytes_accessed=8_000_000, transcendentals=0),
    )(frame, mine, twin, projected, token)


def on_device(core_left, core_right, env_left, env_right, coef_left, coef_right, projected):
    x0, x1 = lax.axis_index("x0"), lax.axis_index("x1")
    core, term = lax.axis_index("core"), lax.axis_index("term")
    swap = [(0, 1), (1, 0)]

    env = env_right.reshape(5, 2, 4, 2, 16, 256)
    env = lax.dynamic_slice(env, (0, x1, 0, core, 0, 0), (5, 1, 4, 1, 16, 256)).reshape(320, 256)
    coefs = jnp.concatenate([coef_left.transpose(1, 0, 2).reshape(15, 128), coef_right.reshape(15, 128)])
    high = lax.reduce_precision(coefs, 8, 7)
    middle = lax.reduce_precision(coefs - high, 8, 7)
    low = coefs - high - middle
    envs = env_left.transpose(1, 0, 2).reshape(20, 256)
    shared = jnp.concatenate(
        [env[:, :128], env[:, 128:], envs[:, :128], envs[:, 128:]]
        + [part.astype(BF16) for part in (high, middle, low)]
        + [jnp.zeros((14, 128), BF16)]
    )
    shared = lax.all_gather(shared, "term")

    points = core_right.reshape(512, 128).T
    points = jnp.pad(points, ((1, 3), (0, 0)))
    mine = lax.dynamic_slice(points, (term * 32, 0), (36, 512))
    windows = jnp.stack([mine[:20], mine[16:]]).reshape(2, 5, 4, 16, 32).transpose(0, 1, 3, 2, 4)
    windows = jnp.broadcast_to(windows.reshape(1, 2, 80, 128), (16, 2, 80, 128)).reshape(32, 80, 128)
    slices = lax.all_to_all(windows, ("lrow", "x1", "x0"), 0, 0, tiled=True).reshape(2560, 128)

    left, rights = left_frames(shared, core_left)
    lefts = lax.all_to_all(jnp.broadcast_to(left[None], (4, 1280, 128)), ("x1", "x0"), 0, 0, tiled=True)
    slices, left = lax.optimization_barrier((slices, left))
    other = lax.ppermute(slices, "core", swap)
    coef = lax.dynamic_slice(rights.reshape(20, 3, 128), (0, 0, term * 32 + x0 * 16), (20, 3, 16)).reshape(20, 48)
    frame, token = right_frames(coef, shared, slices.reshape(160, 16, 128), other.reshape(160, 16, 128))
    token, lefts = lax.optimization_barrier((token, lefts))
    twins = lax.ppermute(lefts, "core", swap)
    part, kept = product(
        frame, lefts.reshape(4, 4, 20, 16, 128), twins.reshape(4, 4, 20, 16, 128), projected, token
    )
    part = lax.all_to_all(part, ("x0", "y"), 0, 0, tiled=True).reshape(2, 2, 16, 4, 16, 128)
    summed = (part[:, 0].astype(F32) + part[:, 1].astype(F32)).reshape(32, 4, 16, 128)
    return (kept.astype(F32) - summed).astype(BF16)


def solution(mesh):
    split = Mesh(mesh.devices.reshape(8, 2, 2, 2, 2, 4), ("lrow",) + RCOL + ("term",))
    return jax.shard_map(
        on_device,
        mesh=split,
        in_specs=(
            P(None, RCOL, None),
            P(RCOL, "lrow", None),
            P("term", "lrow", None),
            P("term", None, None),
            P("term", None, None),
            P("term", None, None),
            P("term", "lrow", RCOL, None),
        ),
        out_specs=P("term", "lrow", RCOL, None),
        check_vma=False,
    )
```

```python
import jax
import jax.numpy as jnp
from jax import lax
from jax.experimental import pallas as pl
from jax.experimental.pallas import tpu as pltpu
from jax.sharding import Mesh, PartitionSpec as P

BF16, F32 = jnp.bfloat16, jnp.float32
RCOL = ("x1", "x0", "y", "core")
VMEM = pl.BlockSpec(memory_space=pltpu.VMEM)
SMEM = pl.BlockSpec(memory_space=pltpu.SMEM)


def unscramble(at, ref, core):
    lane = lax.broadcasted_iota(jnp.int32, (80, 128), 1)
    low, even = lane < 64, (lane // 32) % 2 == 0
    for x in range(4):
        for half in range(2):
            t0, t1, t2, t3 = (
                ref[((half * 4 + m) * 4 + x) * 5 : ((half * 4 + m) * 4 + x + 1) * 5].reshape(80, 128).astype(F32)
                for m in range(4)
            )
            t0, t2 = jnp.where(low, t0, pltpu.roll(t2, 64, 1)), jnp.where(low, pltpu.roll(t0, 64, 1), t2)
            t1, t3 = jnp.where(low, t1, pltpu.roll(t3, 64, 1)), jnp.where(low, pltpu.roll(t1, 64, 1), t3)
            t0, t1 = jnp.where(even, t0, pltpu.roll(t1, 32, 1)), jnp.where(even, pltpu.roll(t0, 96, 1), t1)
            t2, t3 = jnp.where(even, t2, pltpu.roll(t3, 32, 1)), jnp.where(even, pltpu.roll(t2, 96, 1), t3)
            for g, tile in enumerate((t0, t1, t2, t3)):
                tile = tile.astype(BF16)
                for jj in range(5):
                    j = jj * 4 + g
                    if j < 18:
                        top = j * 128 + at * 64 + x * 16
                        core[top : top + 16, half * 128 : half * 128 + 128] = tile[jj * 16 : jj * 16 + 16]


def frames_kernel(
    coef_ref, shared_hbm, mine_hbm, other_hbm, frame_hbm, token_ref, frame, env_ref, mine_ref, other_ref, core, raw, sem
):
    points, ranks, rows, group = 16, 128, 64, 4
    copies = [
        pltpu.make_async_copy(mine_hbm, mine_ref, sem.at[0]),
        pltpu.make_async_copy(other_hbm, other_ref, sem.at[1]),
    ]
    for t in range(4):
        for half in range(2):
            copies.append(
                pltpu.make_async_copy(
                    shared_hbm.at[t, pl.ds(half * 320, 320)],
                    env_ref.at[pl.ds(t * 320, 320), pl.ds(half * 128, 128)],
                    sem.at[2 + t * 2 + half],
                )
            )
    for copy in copies:
        copy.start()
    copies[0].wait()
    unscramble(0, mine_ref, core)
    copies[1].wait()
    unscramble(1, other_ref, core)
    for copy in copies[2:]:
        copy.wait()

    def make(step, carry):
        start = pl.multiple_of(step * group * rows, group * rows)
        env = env_ref[pl.ds(start, group * rows), :]
        raw[...] = lax.dot_general(env, core[...], (((1,), (1,)), ((), ())), preferred_element_type=F32)
        for at in range(group):
            t = step * group + at
            rows_at = slice(at * rows, (at + 1) * rows)
            columns = pl.ds(pl.multiple_of(t * ranks, ranks), ranks)
            for j in range(points):
                frame[j * rows : (j + 1) * rows, columns] = (
                    coef_ref[t, j] * raw[rows_at, (j + 1) * ranks : (j + 2) * ranks]
                    + coef_ref[t, points + j] * raw[rows_at, j * ranks : (j + 1) * ranks]
                    + coef_ref[t, 2 * points + j] * raw[rows_at, (j + 2) * ranks : (j + 3) * ranks]
                ).astype(BF16)
        out(step).start()
        return carry

    def out(step):
        columns = pl.ds(pl.multiple_of(step * group * ranks, group * ranks), group * ranks)
        return pltpu.make_async_copy(frame.at[:, columns], frame_hbm.at[:, columns], sem.at[10 + step])

    lax.fori_loop(0, 5, make, 0)
    token_ref[...] = raw[:8, :128]
    for step in range(5):
        out(step).wait()


def product_kernel(frame_hbm, mine_ref, twin_ref, projected_hbm, token, out_ref, kept_ref, left_ref, frame, sem):
    keep = pltpu.make_async_copy(projected_hbm, kept_ref, sem.at[36])
    pieces = []
    for x in range(4):
        for a in range(4):
            for move, source in enumerate((mine_ref, twin_ref)):
                target = left_ref.at[:, pl.ds(move * 64 + x * 16, 16), pl.ds(a * 128, 128)]
                pieces.append(pltpu.make_async_copy(source.at[x, a], target, sem.at[(x * 4 + a) * 2 + move]))
    chunks = [
        pltpu.make_async_copy(frame_hbm.at[pl.ds(at * 256, 256)], frame.at[pl.ds(at * 256, 256)], sem.at[32 + at])
        for at in range(4)
    ]
    for copy in pieces + chunks + [keep]:
        copy.start()
    for copy in pieces:
        copy.wait()

    def contract(step, carry):
        start = pl.multiple_of(step * 256, 256)
        pltpu.make_async_copy(frame_hbm.at[pl.ds(start, 256)], frame.at[pl.ds(start, 256)], sem.at[32 + step]).wait()
        part = jnp.dot(
            frame[pl.ds(start, 256), :], left_ref[...].reshape(2560, 512), preferred_element_type=F32
        ).astype(BF16)
        for at in range(4):
            for dest in range(4):
                top = at * 64 + dest * 16
                for a in range(4):
                    out_ref[dest, step * 4 + at, a] = part[top : top + 16, a * 128 : (a + 1) * 128]
        return carry

    lax.fori_loop(0, 4, contract, 0)
    keep.wait()


def left_kernel(shared_ref, core_ref, out_ref, coef_ref, tall):
    cores = jnp.swapaxes(core_ref[...].astype(F32), 0, 1).astype(BF16)
    lane = lax.broadcasted_iota(jnp.int32, (80, 128), 1)
    totals = []
    for t in range(4):
        total = (
            shared_ref[t, 680:710].astype(F32) + shared_ref[t, 710:740].astype(F32) + shared_ref[t, 740:770].astype(F32)
        )
        coef_ref[t] = total[15:]
        totals.append(total)
    envs = []
    for a in range(4):
        for t in range(4):
            rows = shared_ref[t, 640:680].astype(F32)
            envs.append(jnp.concatenate([rows[a * 5 : a * 5 + 5], rows[20 + a * 5 : 25 + a * 5]], axis=1))
    envs = jnp.concatenate(envs, axis=0).astype(BF16)
    scales = [[total[k * 5 : k * 5 + 5] for total in totals] * 4 for k in range(3)]
    centre, lower, upper = (jnp.concatenate(part, axis=0) for part in scales)
    lower = jnp.where(lane == 0, 0.0, lower)
    upper = jnp.where(lane == 127, 0.0, upper)
    for r in range(16):
        raw = jnp.dot(envs, cores[r], preferred_element_type=F32)
        tall[pl.ds(r, 80, stride=16), :] = (
            centre * raw + lower * pltpu.roll(raw, 1, 1) + upper * pltpu.roll(raw, 127, 1)
        )
    out_ref[...] = tall[:1280].astype(BF16)


def left_frames(shared, core):
    return pl.pallas_call(
        left_kernel,
        out_shape=(jax.ShapeDtypeStruct((1280, 128), BF16), jax.ShapeDtypeStruct((4, 15, 128), F32)),
        in_specs=[VMEM, VMEM],
        out_specs=(VMEM, VMEM),
        scratch_shapes=[pltpu.VMEM((1296, 128), F32)],
        compiler_params=pltpu.CompilerParams(vmem_limit_bytes=8 << 20),
        cost_estimate=pl.CostEstimate(flops=84_000_000, bytes_accessed=2_000_000, transcendentals=0),
    )(shared, core)


ANYWHERE = pl.BlockSpec(memory_space=pl.ANY)
HBM = pl.BlockSpec(memory_space=pltpu.HBM)


def right_frames(coef, shared, mine, other):
    return pl.pallas_call(
        frames_kernel,
        out_shape=(jax.ShapeDtypeStruct((1024, 2560), BF16), jax.ShapeDtypeStruct((8, 128), F32)),
        in_specs=[SMEM] + [ANYWHERE] * 3,
        out_specs=(HBM, VMEM),
        scratch_shapes=[
            pltpu.VMEM((1024, 2560), BF16),
            pltpu.VMEM((1280, 256), BF16),
            pltpu.VMEM((160, 16, 128), BF16),
            pltpu.VMEM((160, 16, 128), BF16),
            pltpu.VMEM((18 * 128, 256), BF16),
            pltpu.VMEM((256, 18 * 128), F32),
            pltpu.SemaphoreType.DMA((15,)),
        ],
        compiler_params=pltpu.CompilerParams(vmem_limit_bytes=52 << 20),
        cost_estimate=pl.CostEstimate(flops=1_500_000_000, bytes_accessed=8_000_000, transcendentals=0),
    )(coef, shared, mine, other)


def product(frame, mine, twin, projected, token):
    return pl.pallas_call(
        product_kernel,
        out_shape=(
            jax.ShapeDtypeStruct((4, 16, 4, 16, 128), BF16),
            jax.ShapeDtypeStruct((32, 4, 16, 128), BF16),
        ),
        in_specs=[HBM, ANYWHERE, ANYWHERE, HBM, ANYWHERE],
        out_specs=(VMEM, VMEM),
        scratch_shapes=[
            pltpu.VMEM((20, 128, 512), BF16),
            pltpu.VMEM((1024, 2560), BF16),
            pltpu.SemaphoreType.DMA((37,)),
        ],
        compiler_params=pltpu.CompilerParams(vmem_limit_bytes=46 << 20),
        cost_estimate=pl.CostEstimate(flops=2_700_000_000, bytes_accessed=8_000_000, transcendentals=0),
    )(frame, mine, twin, projected, token)


def on_device(core_left, core_right, env_left, env_right, coef_left, coef_right, projected):
    x0, x1 = lax.axis_index("x0"), lax.axis_index("x1")
    core, term = lax.axis_index("core"), lax.axis_index("term")
    swap = [(0, 1), (1, 0)]

    env = env_right.reshape(5, 2, 4, 2, 16, 256)
    env = lax.dynamic_slice(env, (0, x1, 0, core, 0, 0), (5, 1, 4, 1, 16, 256)).reshape(320, 256)
    coefs = jnp.concatenate([coef_left.transpose(1, 0, 2).reshape(15, 128), coef_right.reshape(15, 128)])
    high = lax.reduce_precision(coefs, 8, 7)
    middle = lax.reduce_precision(coefs - high, 8, 7)
    low = coefs - high - middle
    envs = env_left.transpose(1, 0, 2).reshape(20, 256)
    shared = jnp.concatenate(
        [env[:, :128], env[:, 128:], envs[:, :128], envs[:, 128:]]
        + [part.astype(BF16) for part in (high, middle, low)]
        + [jnp.zeros((14, 128), BF16)]
    )
    shared = lax.all_gather(shared, "term")

    points = core_right.reshape(512, 128).T
    points = jnp.pad(points, ((1, 3), (0, 0)))
    mine = lax.dynamic_slice(points, (term * 32, 0), (36, 512))
    windows = jnp.stack([mine[:20], mine[16:]]).reshape(2, 5, 4, 16, 32).transpose(0, 1, 3, 2, 4)
    windows = jnp.broadcast_to(windows.reshape(1, 2, 80, 128), (16, 2, 80, 128)).reshape(32, 80, 128)
    slices = lax.all_to_all(windows, ("lrow", "x1", "x0"), 0, 0, tiled=True).reshape(2560, 128)

    left, rights = left_frames(shared, core_left)
    lefts = lax.all_to_all(jnp.broadcast_to(left[None], (4, 1280, 128)), ("x1", "x0"), 0, 0, tiled=True)
    slices, left = lax.optimization_barrier((slices, left))
    other = lax.ppermute(slices, "core", swap)
    coef = lax.dynamic_slice(rights.reshape(20, 3, 128), (0, 0, term * 32 + x0 * 16), (20, 3, 16)).reshape(20, 48)
    frame, token = right_frames(coef, shared, slices.reshape(160, 16, 128), other.reshape(160, 16, 128))
    token, lefts = lax.optimization_barrier((token, lefts))
    twins = lax.ppermute(lefts, "core", swap)
    part, kept = product(
        frame, lefts.reshape(4, 4, 20, 16, 128), twins.reshape(4, 4, 20, 16, 128), projected, token
    )
    part = lax.all_to_all(part, ("x0", "y"), 0, 0, tiled=True).reshape(2, 2, 16, 4, 16, 128)
    summed = (part[:, 0].astype(F32) + part[:, 1].astype(F32)).reshape(32, 4, 16, 128)
    return (kept.astype(F32) - summed).astype(BF16)


def solution(mesh):
    split = Mesh(mesh.devices.reshape(8, 2, 2, 2, 2, 4), ("lrow",) + RCOL + ("term",))
    return jax.shard_map(
        on_device,
        mesh=split,
        in_specs=(
            P(None, RCOL, None),
            P(RCOL, "lrow", None),
            P("term", "lrow", None),
            P("term", None, None),
            P("term", None, None),
            P("term", None, None),
            P("term", "lrow", RCOL, None),
        ),
        out_specs=P("term", "lrow", RCOL, None),
        check_vma=False,
    )
```

```python
import jax
import jax.numpy as jnp
from jax import lax
from jax.experimental import pallas as pl
from jax.experimental.pallas import tpu as pltpu
from jax.sharding import Mesh, PartitionSpec as P

BF16, F32 = jnp.bfloat16, jnp.float32
RCOL = ("x1", "x0", "y", "core")
VMEM = pl.BlockSpec(memory_space=pltpu.VMEM)
SMEM = pl.BlockSpec(memory_space=pltpu.SMEM)


def unscramble(at, ref, core):
    lane = lax.broadcasted_iota(jnp.int32, (80, 128), 1)
    low, even = lane < 64, (lane // 32) % 2 == 0
    for x in range(4):
        for half in range(2):
            t0, t1, t2, t3 = (
                ref[((half * 4 + m) * 4 + x) * 5 : ((half * 4 + m) * 4 + x + 1) * 5].reshape(80, 128).astype(F32)
                for m in range(4)
            )
            t0, t2 = jnp.where(low, t0, pltpu.roll(t2, 64, 1)), jnp.where(low, pltpu.roll(t0, 64, 1), t2)
            t1, t3 = jnp.where(low, t1, pltpu.roll(t3, 64, 1)), jnp.where(low, pltpu.roll(t1, 64, 1), t3)
            t0, t1 = jnp.where(even, t0, pltpu.roll(t1, 32, 1)), jnp.where(even, pltpu.roll(t0, 96, 1), t1)
            t2, t3 = jnp.where(even, t2, pltpu.roll(t3, 32, 1)), jnp.where(even, pltpu.roll(t2, 96, 1), t3)
            for g, tile in enumerate((t0, t1, t2, t3)):
                tile = tile.astype(BF16)
                for jj in range(5):
                    j = jj * 4 + g
                    if j < 18:
                        top = j * 128 + at * 64 + x * 16
                        core[top : top + 16, half * 128 : half * 128 + 128] = tile[jj * 16 : jj * 16 + 16]


def frames_kernel(
    coef_ref, shared_hbm, mine_hbm, other_hbm, frame_hbm, token_ref, frame, env_ref, mine_ref, other_ref, core, raw, sem
):
    points, ranks, rows, group = 16, 128, 64, 4
    copies = [
        pltpu.make_async_copy(mine_hbm, mine_ref, sem.at[0]),
        pltpu.make_async_copy(other_hbm, other_ref, sem.at[1]),
    ]
    for t in range(4):
        for half in range(2):
            copies.append(
                pltpu.make_async_copy(
                    shared_hbm.at[t, pl.ds(half * 320, 320)],
                    env_ref.at[pl.ds(t * 320, 320), pl.ds(half * 128, 128)],
                    sem.at[2 + t * 2 + half],
                )
            )
    for copy in copies:
        copy.start()
    copies[0].wait()
    unscramble(0, mine_ref, core)
    copies[1].wait()
    unscramble(1, other_ref, core)
    for copy in copies[2:]:
        copy.wait()

    def make(step, carry):
        start = pl.multiple_of(step * group * rows, group * rows)
        env = env_ref[pl.ds(start, group * rows), :]
        raw[...] = lax.dot_general(env, core[...], (((1,), (1,)), ((), ())), preferred_element_type=F32)
        for at in range(group):
            t = step * group + at
            rows_at = slice(at * rows, (at + 1) * rows)
            columns = pl.ds(pl.multiple_of(t * ranks, ranks), ranks)
            for j in range(points):
                frame[j * rows : (j + 1) * rows, columns] = (
                    coef_ref[t, j] * raw[rows_at, (j + 1) * ranks : (j + 2) * ranks]
                    + coef_ref[t, points + j] * raw[rows_at, j * ranks : (j + 1) * ranks]
                    + coef_ref[t, 2 * points + j] * raw[rows_at, (j + 2) * ranks : (j + 3) * ranks]
                ).astype(BF16)
        out(step).start()
        return carry

    def out(step):
        columns = pl.ds(pl.multiple_of(step * group * ranks, group * ranks), group * ranks)
        return pltpu.make_async_copy(frame.at[:, columns], frame_hbm.at[:, columns], sem.at[10 + step])

    lax.fori_loop(0, 5, make, 0)
    token_ref[...] = raw[:8, :128]
    for step in range(5):
        out(step).wait()


def product_kernel(frame_hbm, mine_ref, twin_ref, projected_hbm, token, out_ref, kept_ref, left_ref, frame, sem):
    keep = pltpu.make_async_copy(projected_hbm, kept_ref, sem.at[36])
    pieces = []
    for x in range(4):
        for a in range(4):
            for move, source in enumerate((mine_ref, twin_ref)):
                target = left_ref.at[:, pl.ds(move * 64 + x * 16, 16), pl.ds(a * 128, 128)]
                pieces.append(pltpu.make_async_copy(source.at[x, a], target, sem.at[(x * 4 + a) * 2 + move]))
    chunks = [
        pltpu.make_async_copy(frame_hbm.at[pl.ds(at * 512, 512)], frame.at[pl.ds(at * 512, 512)], sem.at[32 + at])
        for at in range(2)
    ]
    for copy in pieces + chunks + [keep]:
        copy.start()
    for copy in pieces:
        copy.wait()

    def contract(step, carry):
        start = pl.multiple_of(step * 512, 512)
        pltpu.make_async_copy(frame_hbm.at[pl.ds(start, 512)], frame.at[pl.ds(start, 512)], sem.at[32 + step]).wait()
        part = jnp.dot(
            frame[pl.ds(start, 512), :], left_ref[...].reshape(2560, 512), preferred_element_type=F32
        ).astype(BF16)
        for at in range(8):
            for dest in range(4):
                top = at * 64 + dest * 16
                for a in range(4):
                    out_ref[dest, step * 8 + at, a] = part[top : top + 16, a * 128 : (a + 1) * 128]
        return carry

    lax.fori_loop(0, 2, contract, 0)
    keep.wait()


def left_kernel(shared_ref, core_ref, out_ref, coef_ref, tall):
    cores = jnp.swapaxes(core_ref[...].astype(F32), 0, 1).astype(BF16)
    lane = lax.broadcasted_iota(jnp.int32, (80, 128), 1)
    totals = []
    for t in range(4):
        total = (
            shared_ref[t, 680:710].astype(F32) + shared_ref[t, 710:740].astype(F32) + shared_ref[t, 740:770].astype(F32)
        )
        coef_ref[t] = total[15:]
        totals.append(total)
    envs = []
    for a in range(4):
        for t in range(4):
            rows = shared_ref[t, 640:680].astype(F32)
            envs.append(jnp.concatenate([rows[a * 5 : a * 5 + 5], rows[20 + a * 5 : 25 + a * 5]], axis=1))
    envs = jnp.concatenate(envs, axis=0).astype(BF16)
    scales = [[total[k * 5 : k * 5 + 5] for total in totals] * 4 for k in range(3)]
    centre, lower, upper = (jnp.concatenate(part, axis=0) for part in scales)
    lower = jnp.where(lane == 0, 0.0, lower)
    upper = jnp.where(lane == 127, 0.0, upper)
    for r in range(16):
        raw = jnp.dot(envs, cores[r], preferred_element_type=F32)
        tall[pl.ds(r, 80, stride=16), :] = (
            centre * raw + lower * pltpu.roll(raw, 1, 1) + upper * pltpu.roll(raw, 127, 1)
        )
    out_ref[...] = tall[:1280].astype(BF16)


def left_frames(shared, core):
    return pl.pallas_call(
        left_kernel,
        out_shape=(jax.ShapeDtypeStruct((1280, 128), BF16), jax.ShapeDtypeStruct((4, 15, 128), F32)),
        in_specs=[VMEM, VMEM],
        out_specs=(VMEM, VMEM),
        scratch_shapes=[pltpu.VMEM((1296, 128), F32)],
        compiler_params=pltpu.CompilerParams(vmem_limit_bytes=8 << 20),
        cost_estimate=pl.CostEstimate(flops=84_000_000, bytes_accessed=2_000_000, transcendentals=0),
    )(shared, core)


ANYWHERE = pl.BlockSpec(memory_space=pl.ANY)
HBM = pl.BlockSpec(memory_space=pltpu.HBM)


def right_frames(coef, shared, mine, other):
    return pl.pallas_call(
        frames_kernel,
        out_shape=(jax.ShapeDtypeStruct((1024, 2560), BF16), jax.ShapeDtypeStruct((8, 128), F32)),
        in_specs=[SMEM] + [ANYWHERE] * 3,
        out_specs=(HBM, VMEM),
        scratch_shapes=[
            pltpu.VMEM((1024, 2560), BF16),
            pltpu.VMEM((1280, 256), BF16),
            pltpu.VMEM((160, 16, 128), BF16),
            pltpu.VMEM((160, 16, 128), BF16),
            pltpu.VMEM((18 * 128, 256), BF16),
            pltpu.VMEM((256, 18 * 128), F32),
            pltpu.SemaphoreType.DMA((15,)),
        ],
        compiler_params=pltpu.CompilerParams(vmem_limit_bytes=52 << 20),
        cost_estimate=pl.CostEstimate(flops=1_500_000_000, bytes_accessed=8_000_000, transcendentals=0),
    )(coef, shared, mine, other)


def product(frame, mine, twin, projected, token):
    return pl.pallas_call(
        product_kernel,
        out_shape=(
            jax.ShapeDtypeStruct((4, 16, 4, 16, 128), BF16),
            jax.ShapeDtypeStruct((32, 4, 16, 128), BF16),
        ),
        in_specs=[HBM, ANYWHERE, ANYWHERE, HBM, ANYWHERE],
        out_specs=(VMEM, VMEM),
        scratch_shapes=[
            pltpu.VMEM((20, 128, 512), BF16),
            pltpu.VMEM((1024, 2560), BF16),
            pltpu.SemaphoreType.DMA((37,)),
        ],
        compiler_params=pltpu.CompilerParams(vmem_limit_bytes=46 << 20),
        cost_estimate=pl.CostEstimate(flops=2_700_000_000, bytes_accessed=8_000_000, transcendentals=0),
    )(frame, mine, twin, projected, token)


def on_device(core_left, core_right, env_left, env_right, coef_left, coef_right, projected):
    x0, x1 = lax.axis_index("x0"), lax.axis_index("x1")
    core, term = lax.axis_index("core"), lax.axis_index("term")
    swap = [(0, 1), (1, 0)]

    env = env_right.reshape(5, 2, 4, 2, 16, 256)
    env = lax.dynamic_slice(env, (0, x1, 0, core, 0, 0), (5, 1, 4, 1, 16, 256)).reshape(320, 256)
    coefs = jnp.concatenate([coef_left.transpose(1, 0, 2).reshape(15, 128), coef_right.reshape(15, 128)])
    high = lax.reduce_precision(coefs, 8, 7)
    middle = lax.reduce_precision(coefs - high, 8, 7)
    low = coefs - high - middle
    envs = env_left.transpose(1, 0, 2).reshape(20, 256)
    shared = jnp.concatenate(
        [env[:, :128], env[:, 128:], envs[:, :128], envs[:, 128:]]
        + [part.astype(BF16) for part in (high, middle, low)]
        + [jnp.zeros((14, 128), BF16)]
    )
    shared = lax.all_gather(shared, "term")

    points = core_right.reshape(512, 128).T
    points = jnp.pad(points, ((1, 3), (0, 0)))
    mine = lax.dynamic_slice(points, (term * 32, 0), (36, 512))
    windows = jnp.stack([mine[:20], mine[16:]]).reshape(2, 5, 4, 16, 32).transpose(0, 1, 3, 2, 4)
    windows = jnp.broadcast_to(windows.reshape(1, 2, 80, 128), (16, 2, 80, 128)).reshape(32, 80, 128)
    slices = lax.all_to_all(windows, ("lrow", "x1", "x0"), 0, 0, tiled=True).reshape(2560, 128)

    left, rights = left_frames(shared, core_left)
    lefts = lax.all_to_all(jnp.broadcast_to(left[None], (4, 1280, 128)), ("x1", "x0"), 0, 0, tiled=True)
    slices, left = lax.optimization_barrier((slices, left))
    other = lax.ppermute(slices, "core", swap)
    coef = lax.dynamic_slice(rights.reshape(20, 3, 128), (0, 0, term * 32 + x0 * 16), (20, 3, 16)).reshape(20, 48)
    frame, token = right_frames(coef, shared, slices.reshape(160, 16, 128), other.reshape(160, 16, 128))
    token, lefts = lax.optimization_barrier((token, lefts))
    twins = lax.ppermute(lefts, "core", swap)
    part, kept = product(
        frame, lefts.reshape(4, 4, 20, 16, 128), twins.reshape(4, 4, 20, 16, 128), projected, token
    )
    part = lax.all_to_all(part, ("x0", "y"), 0, 0, tiled=True).reshape(2, 2, 16, 4, 16, 128)
    summed = (part[:, 0].astype(F32) + part[:, 1].astype(F32)).reshape(32, 4, 16, 128)
    return (kept.astype(F32) - summed).astype(BF16)


def solution(mesh):
    split = Mesh(mesh.devices.reshape(8, 2, 2, 2, 2, 4), ("lrow",) + RCOL + ("term",))
    return jax.shard_map(
        on_device,
        mesh=split,
        in_specs=(
            P(None, RCOL, None),
            P(RCOL, "lrow", None),
            P("term", "lrow", None),
            P("term", None, None),
            P("term", None, None),
            P("term", None, None),
            P("term", "lrow", RCOL, None),
        ),
        out_specs=P("term", "lrow", RCOL, None),
        check_vma=False,
    )
```
